1024 devices in a mesh: trench: 64 (over y, z_lo, core), tblock: 16 (over z_hi, x).
Axes of the slice: x: 8, y: 8, z: 8 (z_hi: 2, z_lo: 4; z = z_hi * 4 + z_lo), core: 2. Of those that a mesh axis runs over, the one named last changes fastest.
Arguments:
- adjoint_eta: float32 [16, 30, 1024, 512], P('tblock', None, 'trench'), may hold values from -6 to 6
- adjoint_flow: float32 [16, 30, 1024, 512], P('tblock', None, 'trench'), may hold values from -6 to 6
- residual: float32 [16, 64, 64, 4, 32], P('tblock', 'trench'), may hold values from -6 to 6
- sensor_cell: int32 [64, 64, 32], replicated, may hold values from 0 to 8191
- sensor_count: int32 [64, 64], replicated, may hold values from 0 to 32, as said below
- depth_class: int32 [1024, 512], P('trench'), may hold values from 0 to 7
- speed_table: float32 [8], replicated, may hold values from 0.1 to 0.3
- damping: float32 [30], replicated, may hold values from 0.6 to 1
- profile: float32 [30], replicated, may hold values from 0.3 to 1
- band_weight: float32 [8], replicated, may hold values from 0.3 to 1
Outputs:
- uplift_grad: float32 [64, 1024, 512], P(None, ('trench', 'tblock'))
The draws below stay inside these ranges and needn't reach their ends.
Inputs may be any that keep to these rules, and one draw needn't show every extreme that they name: `sensor_cell`: column index inside the owning tile, row times 512 plus column. `sensor_count`: in every draw some owning tile receives 32 live slots from every source tile.
All inputs are finite; a program needn't handle non-finite values.
Results may differ from the reference program's by a relative error of at most 0.0001.
Values sent between devices are 32-bit elements; how exact they have to be, the bound alone decides.
A program may use at most 32 MiB of HBM per device.

```python
import math
import jax
import jax.numpy as jnp
from jax import lax

LEVELS = 30
CX = 16
NY = 512
STEPS = 4
CAP = 32
NCLASS = 8
BAND = 8
NOWN = 64
NWIN = 16
NX = 1024


def draw_sensor_count(key, part):
    first, second, third, fourth = jax.random.split(key, 4)
    base = jax.random.randint(first, (NOWN, NOWN), 0, CAP // 2 + 1, dtype=jnp.int32)
    heavy_owner = jax.random.randint(second, (NOWN,), 0, 4, dtype=jnp.int32) == 0
    higher = jax.random.randint(third, (NOWN, NOWN), CAP // 2, CAP + 1, dtype=jnp.int32)
    counted = jnp.where(heavy_owner[None, :], higher, base)
    full_owner = jax.random.randint(fourth, (), 0, NOWN, dtype=jnp.int32)
    columns = jnp.arange(NOWN, dtype=jnp.int32)
    return jnp.where(columns[None, :] == full_owner, jnp.int32(CAP), counted).astype(jnp.int32)


def plant(array, stream_key, low, high):
    extent = array.shape
    place = [jax.random.randint(jax.random.fold_in(stream_key, axis), (), 0, extent[axis]) for axis in range(len(extent))]
    array = array.at[tuple(place)].set(low)
    longest = extent.index(max(extent))
    place[longest] = (place[longest] + 1) % extent[longest]
    return array.at[tuple(place)].set(high)


def block_levels(stream_key, extent, cuts, smallest, high):
    loudness = 1.0
    for position, blocks in cuts:
        draws = jax.random.uniform(jax.random.fold_in(jax.random.fold_in(stream_key, 6), position), (blocks,), jnp.float32, smallest / len(cuts), high / len(cuts))
        loudness = loudness * jnp.repeat(jnp.exp(draws), extent[position] // blocks).reshape((-1,) + (1,) * (len(extent) - 1 - position))
    return loudness


def gaussian(key, shape, deviation, limit, cuts=(), kind=jnp.bfloat16):
    factor_of = block_levels(key, shape, cuts, -0.22, 0.18) if cuts else 1.0
    drawn = jax.random.normal(key, shape, jnp.float32) * deviation * factor_of
    return jnp.minimum(jnp.maximum(drawn, -limit), limit).astype(kind)


def setup_inputs(seed: int = 0) -> dict:
    arg_keys = jax.random.split(jax.random.key(seed), 11)
    adjoint_eta = gaussian(arg_keys[0], (NWIN, LEVELS, NX, NY), 1.0, 6.0, ((0, 16), (2, 64)), jnp.float32)
    adjoint_flow = gaussian(arg_keys[1], (NWIN, LEVELS, NX, NY), 1.0, 6.0, ((0, 16), (2, 64)), jnp.float32)
    residual = gaussian(arg_keys[2], (NWIN, NOWN, NOWN, STEPS, CAP), 1.0, 6.0, ((0, 16), (1, 64)), jnp.float32)
    sensor_cell = plant(jax.random.randint(arg_keys[3], (NOWN, NOWN, CAP), 0, CX * NY), jax.random.fold_in(arg_keys[3], 1), 0, (CX * NY) - 1).astype(jnp.int32)
    sensor_count = draw_sensor_count(jax.random.fold_in(arg_keys[10], 71), 0)
    depth_class = plant(jax.random.randint(arg_keys[5], (NX, NY), 0, NCLASS), jax.random.fold_in(arg_keys[5], 1), 0, NCLASS - 1).astype(jnp.int32)
    speed_table = jnp.clip(jax.random.uniform(arg_keys[6], (NCLASS,), jnp.float32, 0.1, 0.3), 0.1, 0.3)
    damping = jnp.clip(jax.random.uniform(arg_keys[7], (LEVELS,), jnp.float32, 0.6, 1.0), 0.6, 1.0)
    profile = jnp.clip(jax.random.uniform(arg_keys[8], (LEVELS,), jnp.float32, 0.3, 1.0), 0.3, 1.0)
    band_weight = jnp.clip(jax.random.uniform(arg_keys[9], (BAND,), jnp.float32, 0.3, 1.0), 0.3, 1.0)
    return dict(adjoint_eta=adjoint_eta, adjoint_flow=adjoint_flow, residual=residual, sensor_cell=sensor_cell, sensor_count=sensor_count, depth_class=depth_class, speed_table=speed_table, damping=damping, profile=profile, band_weight=band_weight)


VERT = 0.2

def lookup(depth_class, speed_table):
    classes = jnp.arange(speed_table.shape[0], dtype=jnp.int32)
    return lax.optimization_barrier(jnp.sum(jnp.where(depth_class[..., None] == classes, speed_table, jnp.float32(0.0)), axis=-1))

def advance(widened, displace, momentum, celerity, inject, damping):
    across_pad = jnp.pad(displace, ((0, 0), (0, 0), (1, 1)))
    laplace = widened[:, 2:] + widened[:, :-2] + across_pad[:, :, 2:] + across_pad[:, :, :-2] - 4.0 * displace
    level_pad = jnp.pad(displace, ((1, 1), (0, 0), (0, 0)))
    vertical = level_pad[2:] + level_pad[:-2] - 2.0 * displace
    levels = displace.shape[0]
    bottom = (jnp.arange(levels, dtype=jnp.int32) == levels - 1).astype(jnp.float32)
    momentum = damping[:, None, None] * momentum + celerity[None] * laplace + VERT * vertical + bottom[:, None, None] * inject[None]
    return (displace + momentum, momentum)

def prior(series, band_weight):
    width_band = band_weight.shape[0]
    length = series.shape[0]
    padded = jnp.pad(series, ((0, width_band - 1), (0, 0), (0, 0)))
    result = jnp.zeros_like(series)
    for offset in range(width_band):
        result = result + band_weight[offset] * padded[offset:offset + length]
    return result

def reference(adjoint_eta, adjoint_flow, residual, sensor_cell, sensor_count, depth_class, speed_table, damping, profile, band_weight):
    celerity = lookup(depth_class, speed_table)
    level_scale = 1.0 / math.sqrt(LEVELS)
    slot_ids = jnp.arange(CAP, dtype=jnp.int32)
    alive_mask = (slot_ids[None, None, :] < sensor_count[:, :, None]).astype(jnp.float32)
    owners = jnp.arange(NOWN, dtype=jnp.int32)
    target = (owners[None, :, None] * (CX * NY) + sensor_cell).reshape(-1).astype(jnp.int32)
    series_list = []
    for window in range(NWIN):
        values = residual[window] * alive_mask[:, :, None, :]
        values = jnp.transpose(values, (2, 0, 1, 3)).reshape(STEPS, -1)
        inject_all = jnp.zeros((STEPS, NX * NY), jnp.float32).at[:, target].add(values).reshape(STEPS, NX, NY)
        displace = adjoint_eta[window]
        momentum = adjoint_flow[window]
        pieces = [None] * STEPS
        for step_back in range(STEPS):
            moment = STEPS - 1 - step_back
            widened = jnp.pad(displace, ((0, 0), (1, 1), (0, 0)))
            displace, momentum = advance(widened, displace, momentum, celerity, inject_all[moment], damping)
            pieces[moment] = lax.optimization_barrier(jnp.sum(profile[:, None, None] * momentum, axis=0)) * level_scale
        series_list.extend(pieces)
    series = jnp.stack(series_list, 0)
    return prior(series, band_weight)
```

```python
import functools
import math

import jax
import jax.numpy as jnp
from jax import lax
from jax.experimental import pallas as pl
from jax.experimental.pallas import tpu as pltpu
from jax.sharding import PartitionSpec as P

VERT = 0.2
MESH = pl.DeviceIdType.MESH
LANES = 128
SUB = 8
PHASES = 3
RING = PHASES * SUB
SLOTS = 64


def divisor(count, limit):
    return max(size for size in range(1, limit + 1) if count % size == 0)


def kernel(
    cfg,
    eta,
    flow,
    residual,
    cells,
    counts,
    depth,
    speed,
    damping,
    profile,
    band,
    out,
    disp,
    mom,
    res_buf,
    cell_buf,
    depth_own,
    depth_low,
    depth_high,
    depth_ring,
    coef,
    msg,
    recv,
    onehot_row,
    onehot_col,
    cols,
    inject,
    acc_ref,
    send_rows,
    rows_in,
    edge_in,
    total,
    load_sem,
    depth_send,
    depth_recv,
    res_send,
    res_recv,
    row_send,
    row_recv,
    edge_send,
    edge_recv,
):
    tiles, windows, levels, rows, blocks, steps, cap = cfg
    own = lax.axis_index("trench")
    win = lax.axis_index("tblock")
    f32 = jnp.float32
    reach = steps
    part = steps * blocks
    half = cap // 2

    loads = []
    for j in range(blocks):
        lanes = pl.ds(j * LANES, LANES)
        loads.append(
            pltpu.make_async_copy(
                eta.at[:, :, lanes],
                disp.at[0, j, pl.ds(1, levels), pl.ds(0, rows), :],
                load_sem.at[j],
            )
        )
        loads.append(
            pltpu.make_async_copy(
                flow.at[:, :, lanes], mom.at[j, :, pl.ds(0, rows), :], load_sem.at[blocks + j]
            )
        )
    load_res = pltpu.make_async_copy(residual, res_buf, load_sem.at[2 * blocks])
    load_cell = pltpu.make_async_copy(cells.at[own], cell_buf, load_sem.at[2 * blocks + 1])
    load_depth = pltpu.make_async_copy(depth, depth_own, load_sem.at[2 * blocks + 2])
    load_res.start()
    load_cell.start()
    load_depth.start()
    for copy in loads:
        copy.start()

    edge_in[...] = jnp.zeros_like(edge_in)
    if tiles < SLOTS:
        recv[...] = jnp.zeros_like(recv)

    barrier = pltpu.get_barrier_semaphore()
    after = lax.rem(own + 1, tiles)
    before = lax.rem(own + tiles - 1, tiles)

    def greet(tile, window):
        pl.semaphore_signal(
            barrier, inc=1, device_id={"trench": tile, "tblock": window}, device_id_type=MESH
        )

    greet(after, win)
    greet(before, win)

    def greet_tile(i, carry):
        greet(lax.rem(own + i, tiles), win)
        return carry

    lax.fori_loop(2, tiles - 1, greet_tile, 0)

    def greet_window(i, carry):
        greet(own, lax.rem(win + i, windows))
        return carry

    lax.fori_loop(1, windows, greet_window, 0)

    @pl.when(win < reach)
    def _():
        def step(i, carry):
            greet(before, i)
            return carry

        lax.fori_loop(0, windows, step, 0)

    @pl.when(win >= rows - reach)
    def _():
        def step(i, carry):
            greet(after, i)
            return carry

        lax.fori_loop(0, windows, step, 0)

    zero_tile = jnp.zeros((SUB, LANES), f32)
    for j in range(blocks):
        disp[0, j, :, pl.ds(rows, RING - rows), :] = jnp.zeros(
            (levels + 2, RING - rows, LANES), f32
        )
        mom[j, :, pl.ds(rows, RING - rows), :] = jnp.zeros((levels, RING - rows, LANES), f32)
        for s in range(steps):
            for edge in (0, levels + 1):
                disp[s, j, edge] = jnp.zeros((RING, LANES), f32)
    total[pl.ds(windows * part, RING + SUB), :] = jnp.zeros((RING + SUB, LANES), f32)

    load_res.wait()
    load_cell.wait()
    live_count = counts[pl.ds(own, 1), :]
    slot = lax.broadcasted_iota(jnp.int32, (half, tiles), 0)
    pieces = []
    cell_pieces = []
    for h in range(2):
        live = slot + h * half < live_count
        for t in range(steps):
            pieces.append(
                jnp.where(live, res_buf[pl.ds(t * cap + h * half, half), :], f32(0.0))
            )
        cell = cell_buf[pl.ds(h * half, half), :]
        cell_pieces.append((cell % (blocks * LANES)).astype(f32))
        cell_pieces.append((cell // (blocks * LANES)).astype(f32))
        cell_pieces.append(jnp.zeros((2 * half, tiles), f32))
    msg[:, 0, :] = jnp.transpose(jnp.concatenate(pieces, axis=0))
    msg[:, 1, :] = jnp.transpose(jnp.concatenate(cell_pieces, axis=0))
    recv[pl.ds(own, 1)] = msg[pl.ds(own, 1)]

    load_depth.wait()
    pl.semaphore_wait(barrier, (tiles - 1) + (windows - 1) + 2 * reach)

    to_before = pltpu.make_async_remote_copy(
        src_ref=depth_own.at[pl.ds(0, SUB)],
        dst_ref=depth_low,
        send_sem=depth_send.at[0],
        recv_sem=depth_recv.at[0],
        device_id={"trench": before, "tblock": win},
        device_id_type=MESH,
    )
    to_after = pltpu.make_async_remote_copy(
        src_ref=depth_own.at[pl.ds(rows - SUB, SUB)],
        dst_ref=depth_high,
        send_sem=depth_send.at[1],
        recv_sem=depth_recv.at[1],
        device_id={"trench": after, "tblock": win},
        device_id_type=MESH,
    )
    to_before.start()
    to_after.start()

    def send_residual(i, carry):
        owner = lax.rem(own + i, tiles)
        pltpu.make_async_remote_copy(
            src_ref=msg.at[owner],
            dst_ref=recv.at[own],
            send_sem=res_send,
            recv_sem=res_recv,
            device_id={"trench": owner, "tblock": win},
            device_id_type=MESH,
        ).start()
        return carry

    lax.fori_loop(1, tiles, send_residual, 0)

    to_before.wait_recv()
    to_after.wait_recv()
    sub = lax.broadcasted_iota(jnp.int32, (SUB, LANES), 0)
    lane = lax.broadcasted_iota(jnp.int32, (SUB, LANES), 1)
    for j in range(blocks):
        lanes = pl.ds(j * LANES, LANES)
        depth_ring[j, pl.ds(0, rows), :] = depth_own[:, lanes]
        depth_ring[j, pl.ds(rows, SUB), :] = jnp.where(
            sub < reach, depth_low[:, lanes], depth_high[:, lanes]
        )
    for k in range(PHASES):
        ring_row = sub * PHASES + k
        first = jnp.where(own == 0, 0, 1)
        last = jnp.where(own == tiles - 1, 0, 1)
        valid = jnp.where(ring_row < rows, 1, jnp.where(ring_row < rows + reach, last, first))
        for j in range(blocks):
            classes = depth_ring[j, pl.ds(k, SUB, stride=PHASES), :]
            value = jnp.zeros((SUB, LANES), f32)
            for index in range(speed.shape[0]):
                value = jnp.where(classes == index, speed[index], value)
            value = jnp.where(valid == 1, value, f32(0.0))
            coef[0, j, k] = value
            coef[1, j, k] = 4.0 * value + 2.0 * VERT

    for copy in loads:
        copy.wait()

    def load_disp(s, level):
        if s == 0:
            return [
                [disp[0, j, level + 1, pl.ds(k, SUB, stride=PHASES), :] for k in range(PHASES)]
                for j in range(blocks)
            ]
        return [
            [disp[s, j, level + 1, pl.ds(k * SUB, SUB), :] for k in range(PHASES)]
            for j in range(blocks)
        ]

    at_left = lane == 0
    at_right = lane == LANES - 1

    def update(s, level, below, here, above, acc, source=None):
        damp = damping[level]
        weight = profile[level]
        fresh = []
        for k in range(PHASES):
            turned = [pltpu.roll(here[j][k], 1, axis=1) for j in range(blocks)]
            back = [pltpu.roll(here[j][k], LANES - 1, axis=1) for j in range(blocks)]
            for j in range(blocks):
                left = jnp.where(at_left, turned[j - 1] if j > 0 else f32(0.0), turned[j])
                right = jnp.where(
                    at_right, back[j + 1] if j < blocks - 1 else f32(0.0), back[j]
                )
                up = here[j][k - 1] if k > 0 else pltpu.roll(here[j][PHASES - 1], 1, axis=0)
                down = (
                    here[j][k + 1]
                    if k < PHASES - 1
                    else pltpu.roll(here[j][0], SUB - 1, axis=0)
                )
                if s == 0:
                    old = mom[j, level, pl.ds(k, SUB, stride=PHASES), :]
                else:
                    old = mom[j, level, pl.ds(k * SUB, SUB), :]
                new = (
                    damp * old
                    + coef[0, j, k] * ((left + right) + (up + down))
                    + VERT * (below[j][k] + above[j][k])
                    - coef[1, j, k] * here[j][k]
                )
                if source is not None:
                    new = new + inject[
                        pl.ds((source * PHASES + k) * SUB, SUB), pl.ds(j * LANES, LANES)
                    ]
                fresh.append((j, k, new))
        for j, k, new in fresh:
            if s < steps - 1:
                mom[j, level, pl.ds(k * SUB, SUB), :] = new
                disp[s + 1, j, level + 1, pl.ds(k * SUB, SUB), :] = here[j][k] + new
        acc = list(acc)
        for j, k, new in fresh:
            acc[j * PHASES + k] = acc[j * PHASES + k] + weight * new
        return acc

    def sweep(s, base, count, acc, bottom):
        below = load_disp(s, base - 1)
        here = load_disp(s, base)
        for i in range(count):
            above = load_disp(s, base + i + 1)
            source = steps - 1 - s if bottom and i == count - 1 else None
            acc = update(s, base + i, below, here, above, acc, source)
            below, here = here, above
        return acc

    for s in range(steps):
        ready = levels - 2 - s
        size = divisor(ready, 13)

        def chunk(i, acc, s=s, size=size):
            return tuple(sweep(s, i * size, size, acc, False))

        acc = lax.fori_loop(0, ready // size, chunk, (zero_tile,) * (blocks * PHASES))
        for n, value in enumerate(acc):
            acc_ref[s, n] = value

    wait_all = pltpu.make_async_copy(
        recv.at[pl.ds(0, tiles - 1)], recv.at[pl.ds(0, tiles - 1)], res_recv
    )
    wait_all.wait()
    values = recv[:, 0, :]
    places = recv[:, 1, :]
    values = jnp.transpose(
        jnp.concatenate([values, pltpu.roll(values, LANES // 2, axis=1)], axis=0)
    )
    places = jnp.transpose(
        jnp.concatenate([places, pltpu.roll(places, LANES // 2, axis=1)], axis=0)
    )
    cols[...] = jnp.concatenate([values[: steps * half], places[: 2 * half]], axis=0)
    ring_rows = [(sub * PHASES + k).astype(f32) for k in range(PHASES)]
    columns = lax.broadcasted_iota(jnp.int32, (blocks * LANES, LANES), 0).astype(f32)

    def expand(i, carry):
        lanes = pl.ds(pl.multiple_of(i * LANES, LANES), LANES)
        col = cols[pl.ds(steps * half + i, 1), :]
        row = cols[pl.ds(steps * half + half + i, 1), :]
        match = [row == ring_rows[k] for k in range(PHASES)]
        high, low = [], []
        for t in range(steps):
            value = cols[pl.ds(t * half + i, 1), :]
            coarse = value.astype(jnp.bfloat16).astype(f32)
            fine = value - coarse
            for k in range(PHASES):
                high.append(jnp.where(match[k], coarse, f32(0.0)))
                low.append(jnp.where(match[k], fine, f32(0.0)))
        onehot_row[:, lanes] = jnp.concatenate(high + low, axis=0).astype(jnp.bfloat16)
        onehot_col[:, lanes] = jnp.where(columns == col, f32(1.0), f32(0.0)).astype(jnp.bfloat16)
        return carry

    lax.fori_loop(0, half, expand, 0, unroll=2)
    product = lax.dot_general(
        onehot_row[...],
        onehot_col[...],
        (((1,), (1,)), ((), ())),
        preferred_element_type=f32,
    )
    inject[...] = product[: steps * RING] + product[steps * RING :]

    scale = f32(1.0 / math.sqrt(levels))
    for s in range(steps):
        base = levels - 2 - s
        acc = [acc_ref[s, n] for n in range(blocks * PHASES)]
        acc = sweep(s, base, levels - base, acc, True)
        t = steps - 1 - s
        for j in range(blocks):
            for k in range(PHASES):
                send_rows[pl.ds(k * part + t * blocks + j, SUB, stride=PHASES * part), :] = (
                    acc[j * PHASES + k] * scale
                )

    slot_rows = pl.ds(pl.multiple_of(win * part, part), part)
    edge_copies = []
    for i in range(reach):
        size = part if i < reach // 2 else part // 2
        slot_part = pl.ds(pl.multiple_of(win * part, part), size)
        for ring_row, tile, target in (
            (rows + i, after, i),
            (RING - 1 - i, before, rows - 1 - i),
        ):
            edge_copies.append(
                pltpu.make_async_remote_copy(
                    src_ref=send_rows.at[pl.ds(ring_row * part, size)],
                    dst_ref=edge_in.at[slot_part],
                    send_sem=edge_send.at[len(edge_copies)],
                    recv_sem=edge_recv,
                    device_id={"trench": tile, "tblock": target},
                    device_id_type=MESH,
                )
            )

    def send_row(i, carry):
        target = lax.rem(win + i, windows)
        pltpu.make_async_remote_copy(
            src_ref=send_rows.at[pl.ds(pl.multiple_of(target * part, part), part)],
            dst_ref=rows_in.at[slot_rows],
            send_sem=row_send,
            recv_sem=row_recv,
            device_id={"trench": own, "tblock": target},
            device_id_type=MESH,
        ).start()
        return carry

    lax.fori_loop(1, windows, send_row, 0)
    for copy in edge_copies:
        copy.start()
    rows_in[slot_rows, :] = send_rows[slot_rows, :]

    pltpu.make_async_copy(
        rows_in.at[pl.ds(0, (windows - 1) * part)],
        rows_in.at[pl.ds(0, (windows - 1) * part)],
        row_recv,
    ).wait()

    @pl.when((win < reach // 2) | (win >= rows - reach // 2))
    def _():
        pltpu.make_async_copy(edge_in, edge_in, edge_recv).wait()

    @pl.when(
        ((win >= reach // 2) & (win < reach))
        | ((win < rows - reach // 2) & (win >= rows - reach))
    )
    def _():
        whole = edge_in.at[pl.ds(0, windows * part // 2)]
        pltpu.make_async_copy(whole, whole, edge_recv).wait()

    length = windows * part
    total[pl.ds(0, length), :] = rows_in[...] + edge_in[...]
    result = band[0] * total[pl.ds(0, length), :]
    for offset in range(1, band.shape[0]):
        result = result + band[offset] * total[pl.ds(offset * blocks, length), :]
    out[...] = result

    to_before.wait_send()
    to_after.wait_send()
    pltpu.make_async_copy(
        msg.at[pl.ds(0, tiles - 1)], msg.at[pl.ds(0, tiles - 1)], res_send
    ).wait()
    pltpu.make_async_copy(
        send_rows.at[pl.ds(0, (windows - 1) * part)],
        send_rows.at[pl.ds(0, (windows - 1) * part)],
        row_send,
    ).wait()
    for copy in edge_copies:
        copy.wait_send()


def body(
    tiles,
    windows,
    adjoint_eta,
    adjoint_flow,
    residual,
    sensor_cell,
    sensor_count,
    depth_class,
    speed_table,
    damping,
    profile,
    band_weight,
):
    levels, rows, across = adjoint_eta.shape[1:]
    steps, cap = residual.shape[3:]
    blocks = across // LANES
    part = steps * blocks
    length = windows * part
    f32, i32 = jnp.float32, jnp.int32
    by_owner = jnp.transpose(residual[0, 0], (1, 2, 0)).reshape(steps * cap, tiles)
    cells = jnp.transpose(sensor_cell, (0, 2, 1))
    hbm = pl.BlockSpec(memory_space=pltpu.HBM)
    vmem = pl.BlockSpec(memory_space=pltpu.VMEM)
    smem = pl.BlockSpec(memory_space=pltpu.SMEM)
    dma = pltpu.SemaphoreType.DMA
    result = pl.pallas_call(
        functools.partial(kernel, (tiles, windows, levels, rows, blocks, steps, cap)),
        out_shape=jax.ShapeDtypeStruct((length, LANES), f32),
        in_specs=[hbm, hbm, hbm, hbm, vmem, hbm, smem, smem, smem, smem],
        out_specs=vmem,
        scratch_shapes=[
            pltpu.VMEM((steps, blocks, levels + 2, RING, LANES), f32),
            pltpu.VMEM((blocks, levels, RING, LANES), f32),
            pltpu.VMEM((steps * cap, tiles), f32),
            pltpu.VMEM((cap, tiles), i32),
            pltpu.VMEM((rows, across), i32),
            pltpu.VMEM((SUB, across), i32),
            pltpu.VMEM((SUB, across), i32),
            pltpu.VMEM((blocks, RING, LANES), i32),
            pltpu.VMEM((2, blocks, PHASES, SUB, LANES), f32),
            pltpu.VMEM((tiles, 2, LANES), f32),
            pltpu.VMEM((SLOTS, 2, LANES), f32),
            pltpu.VMEM((2 * steps * RING, SLOTS * cap), jnp.bfloat16),
            pltpu.VMEM((across, SLOTS * cap), jnp.bfloat16),
            pltpu.VMEM((steps * cap // 2 + cap, LANES), f32),
            pltpu.VMEM((steps * RING, across), f32),
            pltpu.VMEM((steps, blocks * PHASES, SUB, LANES), f32),
            pltpu.VMEM((RING * part, LANES), f32),
            pltpu.VMEM((length, LANES), f32),
            pltpu.VMEM((length, LANES), f32),
            pltpu.VMEM((length + RING + SUB, LANES), f32),
            dma((2 * blocks + 3,)),
            dma((2,)),
            dma((2,)),
            dma,
            dma,
            dma,
            dma,
            dma((2 * steps,)),
            dma,
        ],
        compiler_params=pltpu.CompilerParams(
            collective_id=0, has_side_effects=True, vmem_limit_bytes=56 << 20
        ),
        name="adjoint",
    )(
        adjoint_eta[0],
        adjoint_flow[0],
        by_owner,
        cells,
        sensor_count,
        depth_class,
        speed_table,
        damping,
        profile,
        band_weight,
    )
    return result.reshape(windows * steps, 1, across)


def solution(mesh):
    in_specs = (
        P("tblock", None, "trench", None),
        P("tblock", None, "trench", None),
        P("tblock", "trench", None, None, None),
        P(),
        P(),
        P("trench", None),
        P(),
        P(),
        P(),
        P(),
    )
    out_specs = P(None, ("trench", "tblock"), None)
    sizes = mesh.shape
    return jax.shard_map(
        functools.partial(body, sizes["trench"], sizes["tblock"]),
        mesh=mesh,
        in_specs=in_specs,
        out_specs=out_specs,
        check_vma=False,
    )
```

```python
import functools
import math

import jax
import jax.numpy as jnp
from jax import lax
from jax.experimental import pallas as pl
from jax.experimental.pallas import tpu as pltpu
from jax.sharding import PartitionSpec as P

VERT = 0.2
MESH = pl.DeviceIdType.MESH
LANES = 128
SUB = 8
PHASES = 3
RING = PHASES * SUB
SLOTS = 64
TAIL = 32


def kernel(
    cfg,
    eta,
    flow,
    residual,
    cells,
    counts,
    depth,
    speed,
    damping,
    profile,
    total,
    disp,
    mom,
    level_rows,
    weights,
    gammas,
    fields,
    res_buf,
    cell_buf,
    depth_own,
    depth_low,
    depth_high,
    depth_ring,
    celerity,
    msg,
    recv,
    onehot_row,
    onehot_col,
    places,
    cols,
    inject,
    send_rows,
    rows_in,
    edge_in,
    load_sem,
    depth_send,
    depth_recv,
    res_send,
    res_recv,
    row_send,
    row_recv,
    edge_send,
    edge_recv,
    half_in,
    beside_in,
):
    tiles, windows, levels, rows, blocks, steps, cap = cfg
    own = lax.axis_index("trench")
    win = lax.axis_index("tblock")
    f32 = jnp.float32
    reach = steps
    part = steps * blocks
    half = cap // 2
    side = windows // 2

    load_res = pltpu.make_async_copy(residual, res_buf, load_sem.at[0])
    load_cell = pltpu.make_async_copy(cells, cell_buf, load_sem.at[1])
    load_depth = pltpu.make_async_copy(depth, depth_own, load_sem.at[2])
    load_eta = pltpu.make_async_copy(eta, disp, load_sem.at[3])
    load_flow = pltpu.make_async_copy(flow, mom, load_sem.at[4])
    load_res.start()
    load_depth.start()
    load_eta.start()
    load_flow.start()
    load_cell.start()

    edge_in[...] = jnp.zeros_like(edge_in)
    if tiles < SLOTS:
        recv[...] = jnp.zeros_like(recv)

    barrier = pltpu.get_barrier_semaphore()
    after = lax.rem(own + 1, tiles)
    before = lax.rem(own + tiles - 1, tiles)

    def greet(tile, window):
        pl.semaphore_signal(
            barrier, inc=1, device_id={"trench": tile, "tblock": window}, device_id_type=MESH
        )

    def other_tile(i):
        away = lax.div(i + 1, 2)
        return lax.rem(own + tiles // 2 + jnp.where(lax.rem(i, 2) == 1, away, tiles - away), tiles)

    def greet_tile(i, carry):
        greet(other_tile(i), win)
        return carry

    lax.fori_loop(0, tiles - 1, greet_tile, 0)

    my_side = lax.div(win, side)
    my_place = lax.rem(win, side)
    twin = lax.rem(win + side, windows)

    def greet_window(i, carry):
        greet(own, my_side * side + lax.rem(my_place + i, side))
        return carry

    lax.fori_loop(1, side, greet_window, 0)
    greet(own, twin)

    def tell(semaphore, tile, window):
        pl.semaphore_signal(
            semaphore, inc=1, device_id={"trench": tile, "tblock": window}, device_id_type=MESH
        )

    load_res.wait()
    live_count = counts[pl.ds(own, 1), :]
    slot = lax.broadcasted_iota(jnp.int32, (half, tiles), 0)
    pieces = []
    for h in range(2):
        live = slot + h * half < live_count
        for t in range(steps):
            pieces.append(
                jnp.where(live, res_buf[pl.ds(t * cap + h * half, half), :], f32(0.0))
            )
    msg[:, 0, :] = jnp.transpose(jnp.concatenate(pieces, axis=0))
    recv[pl.ds(own, 1)] = msg[pl.ds(own, 1)]
    load_depth.wait()

    to_before = pltpu.make_async_remote_copy(
        src_ref=depth_own.at[pl.ds(0, SUB)],
        dst_ref=depth_low,
        send_sem=depth_send.at[0],
        recv_sem=depth_recv.at[0],
        device_id={"trench": before, "tblock": win},
        device_id_type=MESH,
    )
    to_after = pltpu.make_async_remote_copy(
        src_ref=depth_own.at[pl.ds(rows - SUB, SUB)],
        dst_ref=depth_high,
        send_sem=depth_send.at[1],
        recv_sem=depth_recv.at[1],
        device_id={"trench": after, "tblock": win},
        device_id_type=MESH,
    )

    def send_residual(i, carry):
        owner = other_tile(i)
        pltpu.make_async_remote_copy(
            src_ref=msg.at[owner],
            dst_ref=recv.at[own],
            send_sem=res_send,
            recv_sem=res_recv,
            device_id={"trench": owner, "tblock": win},
            device_id_type=MESH,
        ).start()
        return carry

    def exchange():
        pl.semaphore_wait(barrier, (tiles - 1) + (side - 1) + 1)
        to_before.start()
        to_after.start()
        tell(half_in, own, twin)
        lax.fori_loop(0, tiles - 1, send_residual, 0)

    hurry = (win >= side) & (lax.rem(own, 8) >= min(tiles, 8) // 2)

    @pl.when(hurry)
    def _():
        exchange()

    padded = level_rows.shape[1]
    level_rows[...] = jnp.zeros_like(level_rows)
    for level in range(levels):
        level_rows[0, pl.ds(level, 1), :] = jnp.full((1, LANES), profile[level], f32)
        level_rows[1, pl.ds(level, 1), :] = jnp.full((1, LANES), damping[level], f32)
    weight = level_rows[0]
    damp = level_rows[1]
    inside = lax.broadcasted_iota(jnp.int32, (padded, LANES), 0) < levels

    def vertical(x):
        pair = pltpu.roll(x, 1, axis=0) + pltpu.roll(x, padded - 1, axis=0)
        return jnp.where(inside, VERT * (pair - 2.0 * x), f32(0.0))

    def add(x, y):
        return [
            x[i] + y[i] if i < len(x) and i < len(y) else (x[i] if i < len(x) else y[i])
            for i in range(max(len(x), len(y)))
        ]

    alpha, beta = [weight], []
    sigma = [weight]
    alphas, betas, sigmas = [], [], []
    for _ in range(steps):
        sigmas.append(sigma)
        alpha = [damp * x for x in sigma]
        raised = [jnp.zeros_like(weight)] + sigma
        beta = add(add(beta, [vertical(x) for x in sigma]), raised)
        sigma = add(alpha, beta)
        alphas.append(alpha)
        betas.append(beta)
    slots = [(s, k) for s in range(1, steps + 1) for k in range(s)]
    place = {key: n for n, key in enumerate(slots)}
    on_disp, on_mom = [], []
    count = 0
    for s, k in slots:
        weights[count] = betas[s - 1][k]
        on_disp.append((count, place[s, k]))
        count += 1
        if k < s - 1:
            weights[count] = alphas[s - 1][k]
            on_mom.append((count, place[s, k]))
            count += 1
    weights[count] = weight
    on_disp.append((count, len(slots)))
    weights[count + 1] = damp * weight
    on_mom.append((count + 1, len(slots) + 1))
    gamma_place = {}
    for j in range(steps):
        for k in range(j + 1):
            n = len(gamma_place)
            gamma_place[j, k] = n
            gammas[pl.ds(n, 1), :] = sigmas[j][k][levels - 1 : levels]

    load_eta.wait()
    load_flow.wait()
    n_acc = len(slots) + 2
    zero_tile = jnp.zeros((SUB, LANES), f32)
    for j in range(blocks):
        for n in range(len(slots) + 1):
            fields[n, j, pl.ds(rows, RING - rows), :] = jnp.zeros((RING - rows, LANES), f32)
    for r in range(rows // SUB):
        tile_rows = pl.ds(r * SUB, SUB)

        def contract(level, acc, tile_rows=tile_rows):
            acc = list(acc)
            d = [disp[level, tile_rows, pl.ds(j * LANES, LANES)] for j in range(blocks)]
            m = [mom[level, tile_rows, pl.ds(j * LANES, LANES)] for j in range(blocks)]
            for source, table in ((d, on_disp), (m, on_mom)):
                for row, target in table:
                    w = jnp.broadcast_to(weights[row, pl.ds(level, 1), :], (SUB, LANES))
                    for j in range(blocks):
                        n = target * blocks + j
                        acc[n] = acc[n] + w * source[j]
            return tuple(acc)

        acc = lax.fori_loop(0, levels, contract, (zero_tile,) * (n_acc * blocks), unroll=2)
        for j in range(blocks):
            shared = acc[(len(slots) + 1) * blocks + j]
            for s, k in slots:
                value = acc[place[s, k] * blocks + j]
                fields[place[s, k], j, tile_rows, :] = value + shared if k == s - 1 else value
            fields[len(slots), j, tile_rows, :] = acc[len(slots) * blocks + j]

    load_cell.wait()
    pick = jnp.where(
        lax.broadcasted_iota(jnp.int32, (SUB, tiles), 1) == own, f32(1.0), f32(0.0)
    ).astype(jnp.bfloat16)
    shift = (blocks * LANES).bit_length() - 1
    columns = lax.broadcasted_iota(jnp.int32, (blocks * LANES, LANES), 0).astype(f32)
    for i in range(half):
        sources = []
        for h in range(2):
            sources.append(cell_buf[:, h * half + i, :])
            if tiles < SLOTS:
                sources.append(jnp.zeros((SLOTS - tiles, tiles), jnp.int32))
        cell = jnp.concatenate(sources, axis=0)
        column = cell & (blocks * LANES - 1)
        digits = [cell >> shift, column >> 7, column & (LANES - 1)]
        digits = jnp.concatenate([x.astype(f32) for x in digits], axis=0).astype(jnp.bfloat16)
        found = lax.dot_general(
            pick, digits, (((1,), (1,)), ((), ())), preferred_element_type=f32
        )
        places[pl.ds(half + i, 1), :] = found[:1, :LANES]
        places[pl.ds(i, 1), :] = found[:1, LANES : 2 * LANES] * LANES + found[:1, 2 * LANES :]

    def expand_columns(i, carry):
        lanes = pl.ds(pl.multiple_of(i * LANES, LANES), LANES)
        match = columns == places[pl.ds(i, 1), :]
        onehot_col[:, lanes] = jnp.where(match, f32(1.0), f32(0.0)).astype(jnp.bfloat16)
        return carry

    lax.fori_loop(0, half, expand_columns, 0, unroll=2)

    @pl.when(jnp.logical_not(hurry))
    def _():
        exchange()

    to_before.wait_recv()
    to_after.wait_recv()
    sub = lax.broadcasted_iota(jnp.int32, (SUB, LANES), 0)
    lane = lax.broadcasted_iota(jnp.int32, (SUB, LANES), 1)
    for j in range(blocks):
        lanes = pl.ds(j * LANES, LANES)
        depth_ring[j, pl.ds(0, rows), :] = depth_own[:, lanes]
        depth_ring[j, pl.ds(rows, SUB), :] = jnp.where(
            sub < reach, depth_low[:, lanes], depth_high[:, lanes]
        )
    for k in range(PHASES):
        ring_row = sub * PHASES + k
        first = jnp.where(own == 0, 0, 1)
        last = jnp.where(own == tiles - 1, 0, 1)
        valid = jnp.where(ring_row < rows, 1, jnp.where(ring_row < rows + reach, last, first))
        for j in range(blocks):
            classes = depth_ring[j, pl.ds(k, SUB, stride=PHASES), :]
            value = jnp.zeros((SUB, LANES), f32)
            for index in range(speed.shape[0]):
                value = jnp.where(classes == index, speed[index], value)
            celerity[j, k] = jnp.where(valid == 1, value, f32(0.0))

    pl.semaphore_wait(half_in, 1)
    tell(beside_in, before, win)
    tell(beside_in, after, win)

    pltpu.make_async_copy(
        recv.at[pl.ds(0, tiles - 1)], recv.at[pl.ds(0, tiles - 1)], res_recv
    ).wait()
    values = recv[:, 0, :]
    values = jnp.transpose(
        jnp.concatenate([values, pltpu.roll(values, LANES // 2, axis=1)], axis=0)
    )
    cols[...] = values[: steps * half]
    ring_rows = [(sub * PHASES + k).astype(f32) for k in range(PHASES)]

    def expand(i, carry):
        lanes = pl.ds(pl.multiple_of(i * LANES, LANES), LANES)
        row = places[pl.ds(half + i, 1), :]
        match = [row == ring_rows[k] for k in range(PHASES)]
        high, low = [], []
        for t in range(steps):
            value = cols[pl.ds(t * half + i, 1), :]
            coarse = value.astype(jnp.bfloat16).astype(f32)
            fine = value - coarse
            for k in range(PHASES):
                high.append(jnp.where(match[k], coarse, f32(0.0)))
                low.append(jnp.where(match[k], fine, f32(0.0)))
        onehot_row[:, lanes] = jnp.concatenate(high + low, axis=0).astype(jnp.bfloat16)
        return carry

    lax.fori_loop(0, half, expand, 0, unroll=2)
    product = lax.dot_general(
        onehot_row[...],
        onehot_col[...],
        (((1,), (1,)), ((), ())),
        preferred_element_type=f32,
    )
    inject[...] = product[: steps * RING] + product[steps * RING :]

    at_left = lane == 0
    at_right = lane == LANES - 1
    scale = f32(1.0 / math.sqrt(levels))

    def laplace(x):
        result = [[None] * PHASES for _ in range(blocks)]
        for k in range(PHASES):
            turned = [pltpu.roll(x[j][k], 1, axis=1) for j in range(blocks)]
            back = [pltpu.roll(x[j][k], LANES - 1, axis=1) for j in range(blocks)]
            for j in range(blocks):
                left = jnp.where(at_left, turned[j - 1] if j > 0 else f32(0.0), turned[j])
                right = jnp.where(
                    at_right, back[j + 1] if j < blocks - 1 else f32(0.0), back[j]
                )
                up = x[j][k - 1] if k > 0 else pltpu.roll(x[j][PHASES - 1], 1, axis=0)
                down = x[j][k + 1] if k < PHASES - 1 else pltpu.roll(x[j][0], SUB - 1, axis=0)
                around = (left + right) + (up + down)
                result[j][k] = celerity[j, k] * (around - 4.0 * x[j][k])
        return result

    def field(n):
        return [
            [fields[n, j, pl.ds(k, SUB, stride=PHASES), :] for k in range(PHASES)]
            for j in range(blocks)
        ]

    def plus(x, y):
        return [[x[j][k] + y[j][k] for k in range(PHASES)] for j in range(blocks)]

    def source(s, power):
        value = field(place[s, power])
        for n in range(1, s - power + 1):
            g = gammas[pl.ds(gamma_place[s - n, power], 1), :]
            t = steps - n
            for j in range(blocks):
                for k in range(PHASES):
                    value[j][k] = value[j][k] + g * inject[
                        pl.ds((t * PHASES + k) * SUB, SUB), pl.ds(j * LANES, LANES)
                    ]
        return value

    top = laplace(field(len(slots)))
    for s in range(1, steps + 1):
        value = plus(source(s, s - 1), top)
        for power in range(s - 2, -1, -1):
            value = plus(source(s, power), laplace(value))
        t = steps - s
        for j in range(blocks):
            for k in range(PHASES):
                send_rows[pl.ds(k * part + t * blocks + j, SUB, stride=PHASES * part), :] = (
                    value[j][k] * scale
                )

    slot_rows = pl.ds(pl.multiple_of(win * part, part), part)
    edge_copies = []
    for i in range(reach):
        size = part if i < reach // 2 else part // 2
        slot_part = pl.ds(pl.multiple_of(win * part, part), size)
        for ring_row, tile, target in (
            (rows + i, after, i),
            (RING - 1 - i, before, rows - 1 - i),
        ):
            edge_copies.append(
                pltpu.make_async_remote_copy(
                    src_ref=send_rows.at[pl.ds(ring_row * part, size)],
                    dst_ref=edge_in.at[slot_part],
                    send_sem=edge_send.at[len(edge_copies)],
                    recv_sem=edge_recv,
                    device_id={"trench": tile, "tblock": target},
                    device_id_type=MESH,
                )
            )
    pl.semaphore_wait(beside_in, 2)
    for copy in edge_copies:
        copy.start()

    def send_row(target):
        pltpu.make_async_remote_copy(
            src_ref=send_rows.at[pl.ds(pl.multiple_of(target * part, part), part)],
            dst_ref=rows_in.at[slot_rows],
            send_sem=row_send,
            recv_sem=row_recv,
            device_id={"trench": own, "tblock": target},
            device_id_type=MESH,
        ).start()

    def send_far(i, carry):
        send_row((1 - my_side) * side + lax.rem(my_place + side // 2 + i, side))
        return carry

    def send_near(i, carry):
        send_row(my_side * side + lax.rem(my_place + i, side))
        return carry

    lax.fori_loop(0, side, send_far, 0)
    lax.fori_loop(1, side, send_near, 0)
    rows_in[slot_rows, :] = send_rows[slot_rows, :]

    pltpu.make_async_copy(
        rows_in.at[pl.ds(0, (windows - 1) * part)],
        rows_in.at[pl.ds(0, (windows - 1) * part)],
        row_recv,
    ).wait()

    @pl.when((win < reach // 2) | (win >= rows - reach // 2))
    def _():
        pltpu.make_async_copy(edge_in, edge_in, edge_recv).wait()

    @pl.when(
        ((win >= reach // 2) & (win < reach))
        | ((win < rows - reach // 2) & (win >= rows - reach))
    )
    def _():
        whole = edge_in.at[pl.ds(0, windows * part // 2)]
        pltpu.make_async_copy(whole, whole, edge_recv).wait()

    length = windows * part
    total[pl.ds(0, length), :] = rows_in[...] + edge_in[...]
    total[pl.ds(length, TAIL), :] = jnp.zeros((TAIL, LANES), f32)

    to_before.wait_send()
    to_after.wait_send()
    pltpu.make_async_copy(
        msg.at[pl.ds(0, tiles - 1)], msg.at[pl.ds(0, tiles - 1)], res_send
    ).wait()
    pltpu.make_async_copy(
        send_rows.at[pl.ds(0, (windows - 1) * part)],
        send_rows.at[pl.ds(0, (windows - 1) * part)],
        row_send,
    ).wait()
    for copy in edge_copies:
        copy.wait_send()


def prior(blocks, length, total, band, out):
    result = band[0] * total[pl.ds(0, length), :]
    for offset in range(1, band.shape[0]):
        result = result + band[offset] * total[pl.ds(offset * blocks, length), :]
    out[...] = result


def body(
    tiles,
    windows,
    adjoint_eta,
    adjoint_flow,
    residual,
    sensor_cell,
    sensor_count,
    depth_class,
    speed_table,
    damping,
    profile,
    band_weight,
):
    levels, rows, across = adjoint_eta.shape[1:]
    steps, cap = residual.shape[3:]
    blocks = across // LANES
    part = steps * blocks
    length = windows * part
    f32, i32 = jnp.float32, jnp.int32
    padded = (levels // SUB + 1) * SUB
    pairs = steps * (steps + 1) // 2
    by_owner = jnp.transpose(residual[0, 0], (1, 2, 0)).reshape(steps * cap, tiles)
    cells = jnp.transpose(sensor_cell, (0, 2, 1))
    hbm = pl.BlockSpec(memory_space=pltpu.HBM)
    vmem = pl.BlockSpec(memory_space=pltpu.VMEM)
    smem = pl.BlockSpec(memory_space=pltpu.SMEM)
    dma = pltpu.SemaphoreType.DMA
    total = pl.pallas_call(
        functools.partial(kernel, (tiles, windows, levels, rows, blocks, steps, cap)),
        out_shape=jax.ShapeDtypeStruct((length + TAIL, LANES), f32),
        in_specs=[hbm, hbm, hbm, hbm, vmem, hbm, smem, smem, smem],
        out_specs=vmem,
        scratch_shapes=[
            pltpu.VMEM((levels, rows, across), f32),
            pltpu.VMEM((levels, rows, across), f32),
            pltpu.VMEM((2, padded, LANES), f32),
            pltpu.VMEM((pairs + (steps - 1) * steps // 2 + 2, padded, LANES), f32),
            pltpu.VMEM((2 * SUB, LANES), f32),
            pltpu.VMEM((pairs + 1, blocks, RING, LANES), f32),
            pltpu.VMEM((steps * cap, tiles), f32),
            pltpu.VMEM((tiles, cap, tiles), i32),
            pltpu.VMEM((rows, across), i32),
            pltpu.VMEM((SUB, across), i32),
            pltpu.VMEM((SUB, across), i32),
            pltpu.VMEM((blocks, RING, LANES), i32),
            pltpu.VMEM((blocks, PHASES, SUB, LANES), f32),
            pltpu.VMEM((tiles, 1, LANES), f32),
            pltpu.VMEM((SLOTS, 1, LANES), f32),
            pltpu.VMEM((2 * steps * RING, SLOTS * cap), jnp.bfloat16),
            pltpu.VMEM((across, SLOTS * cap), jnp.bfloat16),
            pltpu.VMEM((cap, LANES), f32),
            pltpu.VMEM((steps * cap // 2, LANES), f32),
            pltpu.VMEM((steps * RING, across), f32),
            pltpu.VMEM((RING * part, LANES), f32),
            pltpu.VMEM((length, LANES), f32),
            pltpu.VMEM((length, LANES), f32),
            dma((5,)),
            dma((2,)),
            dma((2,)),
            dma,
            dma,
            dma,
            dma,
            dma((2 * steps,)),
            dma,
            pltpu.SemaphoreType.REGULAR,
            pltpu.SemaphoreType.REGULAR,
        ],
        compiler_params=pltpu.CompilerParams(
            collective_id=0, has_side_effects=True, vmem_limit_bytes=56 << 20
        ),
        name="adjoint",
    )(
        adjoint_eta[0],
        adjoint_flow[0],
        by_owner,
        cells,
        sensor_count,
        depth_class,
        speed_table,
        damping,
        profile,
    )
    result = pl.pallas_call(
        functools.partial(prior, blocks, length),
        out_shape=jax.ShapeDtypeStruct((length, LANES), f32),
        in_specs=[vmem, smem],
        out_specs=vmem,
        name="prior",
    )(total, band_weight)
    return result.reshape(windows * steps, 1, across)


def solution(mesh):
    in_specs = (
        P("tblock", None, "trench", None),
        P("tblock", None, "trench", None),
        P("tblock", "trench", None, None, None),
        P(),
        P(),
        P("trench", None),
        P(),
        P(),
        P(),
        P(),
    )
    out_specs = P(None, ("trench", "tblock"), None)
    sizes = mesh.shape
    return jax.shard_map(
        functools.partial(body, sizes["trench"], sizes["tblock"]),
        mesh=mesh,
        in_specs=in_specs,
        out_specs=out_specs,
        check_vma=False,
    )
```

```python
import functools
import math

import jax
import jax.numpy as jnp
from jax import lax
from jax.experimental import pallas as pl
from jax.experimental.pallas import tpu as pltpu
from jax.sharding import PartitionSpec as P

VERT = 0.2
MESH = pl.DeviceIdType.MESH
LANES = 128
SUB = 8
PHASES = 3
RING = PHASES * SUB
SLOTS = 64
TAIL = 32


def kernel(
    cfg,
    eta,
    flow,
    residual,
    cells,
    counts_hbm,
    depth,
    speed_hbm,
    damping_hbm,
    profile_hbm,
    total,
    counts,
    speed,
    damping,
    profile,
    disp,
    mom,
    level_rows,
    weights,
    gammas,
    fields,
    res_buf,
    cell_buf,
    depth_own,
    depth_low,
    depth_high,
    depth_ring,
    celerity,
    msg,
    recv,
    onehot_row,
    onehot_col,
    places,
    cols,
    inject,
    from_state,
    send_rows,
    rows_in,
    edge_in,
    load_sem,
    depth_send,
    depth_recv,
    res_send,
    res_recv,
    row_send,
    row_recv,
    edge_send,
    edge_recv,
    half_in,
    beside_in,
):
    tiles, windows, levels, rows, blocks, steps, cap = cfg
    own = lax.axis_index("trench")
    win = lax.axis_index("tblock")
    f32 = jnp.float32
    reach = steps
    part = steps * blocks
    half = cap // 2
    side = windows // 2

    load_res = pltpu.make_async_copy(residual, res_buf, load_sem.at[0])
    load_cell = pltpu.make_async_copy(cells, cell_buf, load_sem.at[1])
    load_depth = pltpu.make_async_copy(depth, depth_own, load_sem.at[2])
    load_eta = pltpu.make_async_copy(eta, disp, load_sem.at[3])
    load_flow = pltpu.make_async_copy(flow, mom, load_sem.at[4])
    load_counts = pltpu.make_async_copy(counts_hbm, counts, load_sem.at[5])
    small = [
        pltpu.make_async_copy(speed_hbm, speed, load_sem.at[6]),
        pltpu.make_async_copy(damping_hbm, damping, load_sem.at[7]),
        pltpu.make_async_copy(profile_hbm, profile, load_sem.at[8]),
    ]
    load_res.start()
    load_counts.start()
    load_depth.start()
    for copy in small:
        copy.start()
    load_eta.start()
    load_flow.start()
    load_cell.start()

    edge_in[...] = jnp.zeros_like(edge_in)
    if tiles < SLOTS:
        recv[...] = jnp.zeros_like(recv)

    barrier = pltpu.get_barrier_semaphore()
    after = lax.rem(own + 1, tiles)
    before = lax.rem(own + tiles - 1, tiles)

    def greet(tile, window):
        pl.semaphore_signal(
            barrier, inc=1, device_id={"trench": tile, "tblock": window}, device_id_type=MESH
        )

    def other_tile(i):
        away = lax.div(i + 1, 2)
        return lax.rem(own + tiles // 2 + jnp.where(lax.rem(i, 2) == 1, away, tiles - away), tiles)

    def greet_tile(i, carry):
        greet(other_tile(i), win)
        return carry

    lax.fori_loop(0, tiles - 1, greet_tile, 0)

    my_side = lax.div(win, side)
    my_place = lax.rem(win, side)
    twin = lax.rem(win + side, windows)

    def greet_window(i, carry):
        greet(own, my_side * side + lax.rem(my_place + i, side))
        return carry

    lax.fori_loop(1, side, greet_window, 0)
    greet(own, twin)

    def tell(semaphore, tile, window):
        pl.semaphore_signal(
            semaphore, inc=1, device_id={"trench": tile, "tblock": window}, device_id_type=MESH
        )

    load_res.wait()
    load_counts.wait()
    live_count = counts[pl.ds(own, 1), :]
    slot = lax.broadcasted_iota(jnp.int32, (half, tiles), 0)
    pieces = []
    for h in range(2):
        live = slot + h * half < live_count
        for t in range(steps):
            pieces.append(
                jnp.where(live, res_buf[pl.ds(t * cap + h * half, half), :], f32(0.0))
            )
    msg[:, 0, :] = jnp.transpose(jnp.concatenate(pieces, axis=0))
    recv[pl.ds(own, 1)] = msg[pl.ds(own, 1)]
    load_depth.wait()

    to_before = pltpu.make_async_remote_copy(
        src_ref=depth_own.at[pl.ds(0, SUB)],
        dst_ref=depth_low,
        send_sem=depth_send.at[0],
        recv_sem=depth_recv.at[0],
        device_id={"trench": before, "tblock": win},
        device_id_type=MESH,
    )
    to_after = pltpu.make_async_remote_copy(
        src_ref=depth_own.at[pl.ds(rows - SUB, SUB)],
        dst_ref=depth_high,
        send_sem=depth_send.at[1],
        recv_sem=depth_recv.at[1],
        device_id={"trench": after, "tblock": win},
        device_id_type=MESH,
    )

    def send_residual(i, carry):
        owner = other_tile(i)
        pltpu.make_async_remote_copy(
            src_ref=msg.at[owner],
            dst_ref=recv.at[own],
            send_sem=res_send,
            recv_sem=res_recv,
            device_id={"trench": owner, "tblock": win},
            device_id_type=MESH,
        ).start()
        return carry

    def exchange():
        pl.semaphore_wait(barrier, (tiles - 1) + (side - 1) + 1)
        to_before.start()
        to_after.start()
        tell(half_in, own, twin)
        lax.fori_loop(0, tiles - 1, send_residual, 0)

    hurry = (win >= side) & (lax.rem(own, 8) >= min(tiles, 8) // 2)

    @pl.when(hurry)
    def _():
        exchange()

    for copy in small:
        copy.wait()
    padded = level_rows.shape[1]
    level_rows[...] = jnp.zeros_like(level_rows)
    for level in range(levels):
        level_rows[0, pl.ds(level, 1), :] = jnp.full((1, LANES), profile[level], f32)
        level_rows[1, pl.ds(level, 1), :] = jnp.full((1, LANES), damping[level], f32)
    weight = level_rows[0]
    damp = level_rows[1]
    inside = lax.broadcasted_iota(jnp.int32, (padded, LANES), 0) < levels

    def vertical(x):
        pair = pltpu.roll(x, 1, axis=0) + pltpu.roll(x, padded - 1, axis=0)
        return jnp.where(inside, VERT * (pair - 2.0 * x), f32(0.0))

    def add(x, y):
        return [
            x[i] + y[i] if i < len(x) and i < len(y) else (x[i] if i < len(x) else y[i])
            for i in range(max(len(x), len(y)))
        ]

    alpha, beta = [weight], []
    sigma = [weight]
    alphas, betas, sigmas = [], [], []
    for _ in range(steps):
        sigmas.append(sigma)
        alpha = [damp * x for x in sigma]
        raised = [jnp.zeros_like(weight)] + sigma
        beta = add(add(beta, [vertical(x) for x in sigma]), raised)
        sigma = add(alpha, beta)
        alphas.append(alpha)
        betas.append(beta)
    slots = [(s, k) for s in range(1, steps + 1) for k in range(s)]
    place = {key: n for n, key in enumerate(slots)}
    on_disp, on_mom = [], []
    count = 0
    for s, k in slots:
        weights[count] = betas[s - 1][k]
        on_disp.append((count, place[s, k]))
        count += 1
        if k < s - 1:
            weights[count] = alphas[s - 1][k]
            on_mom.append((count, place[s, k]))
            count += 1
    weights[count] = weight
    on_disp.append((count, len(slots)))
    weights[count + 1] = damp * weight
    on_mom.append((count + 1, len(slots) + 1))
    gamma_place = {}
    for j in range(steps):
        for k in range(j + 1):
            n = len(gamma_place)
            gamma_place[j, k] = n
            gammas[pl.ds(n, 1), :] = sigmas[j][k][levels - 1 : levels]

    load_eta.wait()
    load_flow.wait()
    n_acc = len(slots) + 2
    zero_tile = jnp.zeros((SUB, LANES), f32)
    for j in range(blocks):
        for n in range(len(slots) + 1):
            fields[n, j, pl.ds(rows, RING - rows), :] = jnp.zeros((RING - rows, LANES), f32)
    for r in range(rows // SUB):
        tile_rows = pl.ds(r * SUB, SUB)

        def contract(level, acc, tile_rows=tile_rows):
            acc = list(acc)
            d = [disp[level, tile_rows, pl.ds(j * LANES, LANES)] for j in range(blocks)]
            m = [mom[level, tile_rows, pl.ds(j * LANES, LANES)] for j in range(blocks)]
            for source, table in ((d, on_disp), (m, on_mom)):
                for row, target in table:
                    w = jnp.broadcast_to(weights[row, pl.ds(level, 1), :], (SUB, LANES))
                    for j in range(blocks):
                        n = target * blocks + j
                        acc[n] = acc[n] + w * source[j]
            return tuple(acc)

        acc = lax.fori_loop(0, levels, contract, (zero_tile,) * (n_acc * blocks), unroll=2)
        for j in range(blocks):
            shared = acc[(len(slots) + 1) * blocks + j]
            for s, k in slots:
                value = acc[place[s, k] * blocks + j]
                fields[place[s, k], j, tile_rows, :] = value + shared if k == s - 1 else value
            fields[len(slots), j, tile_rows, :] = acc[len(slots) * blocks + j]

    load_cell.wait()
    pick = jnp.where(
        lax.broadcasted_iota(jnp.int32, (SUB, tiles), 1) == own, f32(1.0), f32(0.0)
    ).astype(jnp.bfloat16)
    shift = (blocks * LANES).bit_length() - 1
    columns = lax.broadcasted_iota(jnp.int32, (blocks * LANES, LANES), 0).astype(f32)
    for i in range(half):
        sources = []
        for h in range(2):
            sources.append(cell_buf[:, h * half + i, :])
            if tiles < SLOTS:
                sources.append(jnp.zeros((SLOTS - tiles, tiles), jnp.int32))
        cell = jnp.concatenate(sources, axis=0)
        column = cell & (blocks * LANES - 1)
        digits = [cell >> shift, column >> 7, column & (LANES - 1)]
        digits = jnp.concatenate([x.astype(f32) for x in digits], axis=0).astype(jnp.bfloat16)
        found = lax.dot_general(
            pick, digits, (((1,), (1,)), ((), ())), preferred_element_type=f32
        )
        places[pl.ds(half + i, 1), :] = found[:1, :LANES]
        places[pl.ds(i, 1), :] = found[:1, LANES : 2 * LANES] * LANES + found[:1, 2 * LANES :]

    def expand_columns(i, carry):
        lanes = pl.ds(pl.multiple_of(i * LANES, LANES), LANES)
        match = columns == places[pl.ds(i, 1), :]
        onehot_col[:, lanes] = jnp.where(match, f32(1.0), f32(0.0)).astype(jnp.bfloat16)
        return carry

    lax.fori_loop(0, half, expand_columns, 0, unroll=2)

    @pl.when(jnp.logical_not(hurry))
    def _():
        exchange()

    pl.semaphore_wait(half_in, 1)
    tell(beside_in, before, win)
    tell(beside_in, after, win)
    to_before.wait_recv()
    to_after.wait_recv()
    sub = lax.broadcasted_iota(jnp.int32, (SUB, LANES), 0)
    lane = lax.broadcasted_iota(jnp.int32, (SUB, LANES), 1)
    for j in range(blocks):
        lanes = pl.ds(j * LANES, LANES)
        depth_ring[j, pl.ds(0, rows), :] = depth_own[:, lanes]
        depth_ring[j, pl.ds(rows, SUB), :] = jnp.where(
            sub < reach, depth_low[:, lanes], depth_high[:, lanes]
        )
    for k in range(PHASES):
        ring_row = sub * PHASES + k
        first = jnp.where(own == 0, 0, 1)
        last = jnp.where(own == tiles - 1, 0, 1)
        valid = jnp.where(ring_row < rows, 1, jnp.where(ring_row < rows + reach, last, first))
        for j in range(blocks):
            classes = depth_ring[j, pl.ds(k, SUB, stride=PHASES), :]
            value = jnp.zeros((SUB, LANES), f32)
            for index in range(speed.shape[0]):
                value = jnp.where(classes == index, speed[index], value)
            celerity[j, k] = jnp.where(valid == 1, value, f32(0.0))

    at_left = lane == 0
    at_right = lane == LANES - 1
    scale = f32(1.0 / math.sqrt(levels))

    def laplace(x):
        result = [[None] * PHASES for _ in range(blocks)]
        for k in range(PHASES):
            turned = [pltpu.roll(x[j][k], 1, axis=1) for j in range(blocks)]
            back = [pltpu.roll(x[j][k], LANES - 1, axis=1) for j in range(blocks)]
            for j in range(blocks):
                left = jnp.where(at_left, turned[j - 1] if j > 0 else f32(0.0), turned[j])
                right = jnp.where(
                    at_right, back[j + 1] if j < blocks - 1 else f32(0.0), back[j]
                )
                up = x[j][k - 1] if k > 0 else pltpu.roll(x[j][PHASES - 1], 1, axis=0)
                down = x[j][k + 1] if k < PHASES - 1 else pltpu.roll(x[j][0], SUB - 1, axis=0)
                around = (left + right) + (up + down)
                result[j][k] = celerity[j, k] * (around - 4.0 * x[j][k])
        return result

    def field(n):
        return [
            [fields[n, j, pl.ds(k, SUB, stride=PHASES), :] for k in range(PHASES)]
            for j in range(blocks)
        ]

    def plus(x, y):
        return [[x[j][k] + y[j][k] for k in range(PHASES)] for j in range(blocks)]

    top = laplace(field(len(slots)))
    for s in range(1, steps + 1):
        value = plus(field(place[s, s - 1]), top)
        for power in range(s - 2, -1, -1):
            value = plus(field(place[s, power]), laplace(value))
        for j in range(blocks):
            for k in range(PHASES):
                from_state[s - 1, j, k] = value[j][k]

    pltpu.make_async_copy(
        recv.at[pl.ds(0, tiles - 1)], recv.at[pl.ds(0, tiles - 1)], res_recv
    ).wait()
    values = recv[:, 0, :]
    values = jnp.transpose(
        jnp.concatenate([values, pltpu.roll(values, LANES // 2, axis=1)], axis=0)
    )
    cols[...] = values[: steps * half]
    ring_rows = [(sub * PHASES + k).astype(f32) for k in range(PHASES)]

    def expand(i, carry):
        lanes = pl.ds(pl.multiple_of(i * LANES, LANES), LANES)
        row = places[pl.ds(half + i, 1), :]
        match = [row == ring_rows[k] for k in range(PHASES)]
        high, low = [], []
        for t in range(steps):
            value = cols[pl.ds(t * half + i, 1), :]
            coarse = value.astype(jnp.bfloat16).astype(f32)
            fine = value - coarse
            for k in range(PHASES):
                high.append(jnp.where(match[k], coarse, f32(0.0)))
                low.append(jnp.where(match[k], fine, f32(0.0)))
        onehot_row[:, lanes] = jnp.concatenate(high + low, axis=0).astype(jnp.bfloat16)
        return carry

    lax.fori_loop(0, half, expand, 0, unroll=4)
    product = lax.dot_general(
        onehot_row[...],
        onehot_col[...],
        (((1,), (1,)), ((), ())),
        preferred_element_type=f32,
    )
    inject[...] = product[: steps * RING] + product[steps * RING :]

    def source(s, power):
        value = [[None] * PHASES for _ in range(blocks)]
        for n in range(1, s - power + 1):
            g = gammas[pl.ds(gamma_place[s - n, power], 1), :]
            t = steps - n
            for j in range(blocks):
                for k in range(PHASES):
                    term = g * inject[
                        pl.ds((t * PHASES + k) * SUB, SUB), pl.ds(j * LANES, LANES)
                    ]
                    value[j][k] = term if value[j][k] is None else value[j][k] + term
        return value

    for s in range(1, steps + 1):
        value = source(s, s - 1)
        for power in range(s - 2, -1, -1):
            value = plus(source(s, power), laplace(value))
        t = steps - s
        for j in range(blocks):
            for k in range(PHASES):
                send_rows[pl.ds(k * part + t * blocks + j, SUB, stride=PHASES * part), :] = (
                    value[j][k] + from_state[s - 1, j, k]
                ) * scale

    slot_rows = pl.ds(pl.multiple_of(win * part, part), part)
    edge_copies = []
    for i in range(reach):
        size = part if i < reach // 2 else part // 2
        slot_part = pl.ds(pl.multiple_of(win * part, part), size)
        for ring_row, tile, target in (
            (rows + i, after, i),
            (RING - 1 - i, before, rows - 1 - i),
        ):
            edge_copies.append(
                pltpu.make_async_remote_copy(
                    src_ref=send_rows.at[pl.ds(ring_row * part, size)],
                    dst_ref=edge_in.at[slot_part],
                    send_sem=edge_send.at[len(edge_copies)],
                    recv_sem=edge_recv,
                    device_id={"trench": tile, "tblock": target},
                    device_id_type=MESH,
                )
            )
    def send_row(target):
        pltpu.make_async_remote_copy(
            src_ref=send_rows.at[pl.ds(pl.multiple_of(target * part, part), part)],
            dst_ref=rows_in.at[slot_rows],
            send_sem=row_send,
            recv_sem=row_recv,
            device_id={"trench": own, "tblock": target},
            device_id_type=MESH,
        ).start()

    def send_far(i, carry):
        send_row((1 - my_side) * side + lax.rem(my_place + side // 2 + i, side))
        return carry

    def send_near(i, carry):
        send_row(my_side * side + lax.rem(my_place + i, side))
        return carry

    lax.fori_loop(0, side, send_far, 0)
    pl.semaphore_wait(beside_in, 2)
    for copy in edge_copies:
        copy.start()
    lax.fori_loop(1, side, send_near, 0)
    rows_in[slot_rows, :] = send_rows[slot_rows, :]

    pltpu.make_async_copy(
        rows_in.at[pl.ds(0, (windows - 1) * part)],
        rows_in.at[pl.ds(0, (windows - 1) * part)],
        row_recv,
    ).wait()

    @pl.when((win < reach // 2) | (win >= rows - reach // 2))
    def _():
        pltpu.make_async_copy(edge_in, edge_in, edge_recv).wait()

    @pl.when(
        ((win >= reach // 2) & (win < reach))
        | ((win < rows - reach // 2) & (win >= rows - reach))
    )
    def _():
        whole = edge_in.at[pl.ds(0, windows * part // 2)]
        pltpu.make_async_copy(whole, whole, edge_recv).wait()

    length = windows * part
    total[pl.ds(0, length), :] = rows_in[...] + edge_in[...]
    total[pl.ds(length, TAIL), :] = jnp.zeros((TAIL, LANES), f32)

    to_before.wait_send()
    to_after.wait_send()
    pltpu.make_async_copy(
        msg.at[pl.ds(0, tiles - 1)], msg.at[pl.ds(0, tiles - 1)], res_send
    ).wait()
    pltpu.make_async_copy(
        send_rows.at[pl.ds(0, (windows - 1) * part)],
        send_rows.at[pl.ds(0, (windows - 1) * part)],
        row_send,
    ).wait()
    for copy in edge_copies:
        copy.wait_send()


def prior(blocks, length, total, band, out):
    result = band[0] * total[pl.ds(0, length), :]
    for offset in range(1, band.shape[0]):
        result = result + band[offset] * total[pl.ds(offset * blocks, length), :]
    out[...] = result


def body(
    tiles,
    windows,
    adjoint_eta,
    adjoint_flow,
    residual,
    sensor_cell,
    sensor_count,
    depth_class,
    speed_table,
    damping,
    profile,
    band_weight,
):
    levels, rows, across = adjoint_eta.shape[1:]
    steps, cap = residual.shape[3:]
    blocks = across // LANES
    part = steps * blocks
    length = windows * part
    f32, i32 = jnp.float32, jnp.int32
    padded = (levels // SUB + 1) * SUB
    pairs = steps * (steps + 1) // 2
    by_owner = jnp.transpose(residual[0, 0], (1, 2, 0)).reshape(steps * cap, tiles)
    cells = jnp.transpose(sensor_cell, (0, 2, 1))
    hbm = pl.BlockSpec(memory_space=pltpu.HBM)
    vmem = pl.BlockSpec(memory_space=pltpu.VMEM)
    smem = pl.BlockSpec(memory_space=pltpu.SMEM)
    dma = pltpu.SemaphoreType.DMA
    total = pl.pallas_call(
        functools.partial(kernel, (tiles, windows, levels, rows, blocks, steps, cap)),
        out_shape=jax.ShapeDtypeStruct((length + TAIL, LANES), f32),
        in_specs=[hbm] * 9,
        out_specs=vmem,
        scratch_shapes=[
            pltpu.VMEM(sensor_count.shape, i32),
            pltpu.SMEM(speed_table.shape, f32),
            pltpu.SMEM(damping.shape, f32),
            pltpu.SMEM(profile.shape, f32),
            pltpu.VMEM((levels, rows, across), f32),
            pltpu.VMEM((levels, rows, across), f32),
            pltpu.VMEM((2, padded, LANES), f32),
            pltpu.VMEM((pairs + (steps - 1) * steps // 2 + 2, padded, LANES), f32),
            pltpu.VMEM((2 * SUB, LANES), f32),
            pltpu.VMEM((pairs + 1, blocks, RING, LANES), f32),
            pltpu.VMEM((steps * cap, tiles), f32),
            pltpu.VMEM((tiles, cap, tiles), i32),
            pltpu.VMEM((rows, across), i32),
            pltpu.VMEM((SUB, across), i32),
            pltpu.VMEM((SUB, across), i32),
            pltpu.VMEM((blocks, RING, LANES), i32),
            pltpu.VMEM((blocks, PHASES, SUB, LANES), f32),
            pltpu.VMEM((tiles, 1, LANES), f32),
            pltpu.VMEM((SLOTS, 1, LANES), f32),
            pltpu.VMEM((2 * steps * RING, SLOTS * cap), jnp.bfloat16),
            pltpu.VMEM((across, SLOTS * cap), jnp.bfloat16),
            pltpu.VMEM((cap, LANES), f32),
            pltpu.VMEM((steps * cap // 2, LANES), f32),
            pltpu.VMEM((steps * RING, across), f32),
            pltpu.VMEM((steps, blocks, PHASES, SUB, LANES), f32),
            pltpu.VMEM((RING * part, LANES), f32),
            pltpu.VMEM((length, LANES), f32),
            pltpu.VMEM((length, LANES), f32),
            dma((9,)),
            dma((2,)),
            dma((2,)),
            dma,
            dma,
            dma,
            dma,
            dma((2 * steps,)),
            dma,
            pltpu.SemaphoreType.REGULAR,
            pltpu.SemaphoreType.REGULAR,
        ],
        compiler_params=pltpu.CompilerParams(
            collective_id=0, has_side_effects=True, vmem_limit_bytes=56 << 20
        ),
        name="adjoint",
    )(
        adjoint_eta[0],
        adjoint_flow[0],
        by_owner,
        cells,
        sensor_count,
        depth_class,
        speed_table,
        damping,
        profile,
    )
    result = pl.pallas_call(
        functools.partial(prior, blocks, length),
        out_shape=jax.ShapeDtypeStruct((length, LANES), f32),
        in_specs=[vmem, smem],
        out_specs=vmem,
        name="prior",
    )(total, band_weight)
    return result.reshape(windows * steps, 1, across)


def solution(mesh):
    in_specs = (
        P("tblock", None, "trench", None),
        P("tblock", None, "trench", None),
        P("tblock", "trench", None, None, None),
        P(),
        P(),
        P("trench", None),
        P(),
        P(),
        P(),
        P(),
    )
    out_specs = P(None, ("trench", "tblock"), None)
    sizes = mesh.shape
    return jax.shard_map(
        functools.partial(body, sizes["trench"], sizes["tblock"]),
        mesh=mesh,
        in_specs=in_specs,
        out_specs=out_specs,
        check_vma=False,
    )
```

```python
import functools
import math

import jax
import jax.numpy as jnp
from jax import lax
from jax.experimental import pallas as pl
from jax.experimental.pallas import tpu as pltpu
from jax.sharding import PartitionSpec as P

VERT = 0.2
MESH = pl.DeviceIdType.MESH
LANES = 128
SUB = 8
PHASES = 3
RING = PHASES * SUB
SLOTS = 64
TAIL = 32


def kernel(
    cfg,
    eta,
    flow,
    residual,
    cells,
    counts_hbm,
    depth,
    speed_hbm,
    damping_hbm,
    profile_hbm,
    total,
    counts,
    speed,
    damping,
    profile,
    disp,
    mom,
    level_rows,
    weights,
    gammas,
    fields,
    res_buf,
    cell_buf,
    depth_own,
    depth_low,
    depth_high,
    depth_ring,
    celerity,
    msg,
    recv,
    onehot_row,
    onehot_col,
    places,
    cols,
    inject,
    from_state,
    send_rows,
    rows_in,
    edge_in,
    load_sem,
    depth_send,
    depth_recv,
    res_send,
    res_recv,
    row_send,
    row_recv,
    edge_send,
    edge_recv,
    half_in,
    beside_in,
):
    tiles, windows, levels, rows, blocks, steps, cap = cfg
    own = lax.axis_index("trench")
    win = lax.axis_index("tblock")
    f32 = jnp.float32
    reach = steps
    part = steps * blocks
    half = cap // 2
    side = windows // 2

    load_res = pltpu.make_async_copy(residual, res_buf, load_sem.at[0])
    load_cell = pltpu.make_async_copy(cells, cell_buf, load_sem.at[1])
    load_depth = pltpu.make_async_copy(depth, depth_own, load_sem.at[2])
    load_eta = pltpu.make_async_copy(eta, disp, load_sem.at[3])
    load_flow = pltpu.make_async_copy(flow, mom, load_sem.at[4])
    load_counts = pltpu.make_async_copy(counts_hbm, counts, load_sem.at[5])
    small = [
        pltpu.make_async_copy(speed_hbm, speed, load_sem.at[6]),
        pltpu.make_async_copy(damping_hbm, damping, load_sem.at[7]),
        pltpu.make_async_copy(profile_hbm, profile, load_sem.at[8]),
    ]
    load_res.start()
    load_counts.start()
    load_depth.start()
    for copy in small:
        copy.start()

    edge_in[...] = jnp.zeros_like(edge_in)
    if tiles < SLOTS:
        recv[...] = jnp.zeros_like(recv)

    barrier = pltpu.get_barrier_semaphore()
    after = lax.rem(own + 1, tiles)
    before = lax.rem(own + tiles - 1, tiles)

    def greet(tile, window):
        pl.semaphore_signal(
            barrier, inc=1, device_id={"trench": tile, "tblock": window}, device_id_type=MESH
        )

    def other_tile(i):
        away = lax.div(i + 1, 2)
        return lax.rem(own + tiles // 2 + jnp.where(lax.rem(i, 2) == 1, away, tiles - away), tiles)

    def greet_tile(i, carry):
        greet(other_tile(i), win)
        return carry

    lax.fori_loop(0, tiles - 1, greet_tile, 0)

    my_side = lax.div(win, side)
    my_place = lax.rem(win, side)
    twin = lax.rem(win + side, windows)

    def greet_window(i, carry):
        greet(own, my_side * side + lax.rem(my_place + i, side))
        return carry

    lax.fori_loop(1, side, greet_window, 0)
    greet(own, twin)

    def tell(semaphore, tile, window):
        pl.semaphore_signal(
            semaphore, inc=1, device_id={"trench": tile, "tblock": window}, device_id_type=MESH
        )

    load_eta.start()
    load_flow.start()
    load_cell.start()

    load_res.wait()
    load_counts.wait()
    live_count = counts[pl.ds(own, 1), :]
    slot = lax.broadcasted_iota(jnp.int32, (half, tiles), 0)
    pieces = []
    for h in range(2):
        live = slot + h * half < live_count
        for t in range(steps):
            pieces.append(
                jnp.where(live, res_buf[pl.ds(t * cap + h * half, half), :], f32(0.0))
            )
    msg[:, 0, :] = jnp.transpose(jnp.concatenate(pieces, axis=0))
    recv[pl.ds(own, 1)] = msg[pl.ds(own, 1)]
    load_depth.wait()

    to_before = pltpu.make_async_remote_copy(
        src_ref=depth_own.at[pl.ds(0, SUB)],
        dst_ref=depth_low,
        send_sem=depth_send.at[0],
        recv_sem=depth_recv.at[0],
        device_id={"trench": before, "tblock": win},
        device_id_type=MESH,
    )
    to_after = pltpu.make_async_remote_copy(
        src_ref=depth_own.at[pl.ds(rows - SUB, SUB)],
        dst_ref=depth_high,
        send_sem=depth_send.at[1],
        recv_sem=depth_recv.at[1],
        device_id={"trench": after, "tblock": win},
        device_id_type=MESH,
    )

    def send_residual(i, carry):
        owner = other_tile(i)
        pltpu.make_async_remote_copy(
            src_ref=msg.at[owner],
            dst_ref=recv.at[own],
            send_sem=res_send,
            recv_sem=res_recv,
            device_id={"trench": owner, "tblock": win},
            device_id_type=MESH,
        ).start()
        return carry

    def exchange():
        pl.semaphore_wait(barrier, (tiles - 1) + (side - 1) + 1)
        to_before.start()
        to_after.start()
        tell(half_in, own, twin)
        lax.fori_loop(0, tiles - 1, send_residual, 0)

    hurry = (win >= side) & (lax.rem(own, 8) >= min(tiles, 8) // 2)

    @pl.when(hurry)
    def _():
        exchange()

    for copy in small:
        copy.wait()
    padded = level_rows.shape[1]
    level_rows[...] = jnp.zeros_like(level_rows)
    for level in range(levels):
        level_rows[0, pl.ds(level, 1), :] = jnp.full((1, LANES), profile[level], f32)
        level_rows[1, pl.ds(level, 1), :] = jnp.full((1, LANES), damping[level], f32)
    weight = level_rows[0]
    damp = level_rows[1]
    inside = lax.broadcasted_iota(jnp.int32, (padded, LANES), 0) < levels

    def vertical(x):
        pair = pltpu.roll(x, 1, axis=0) + pltpu.roll(x, padded - 1, axis=0)
        return jnp.where(inside, VERT * (pair - 2.0 * x), f32(0.0))

    def add(x, y):
        return [
            x[i] + y[i] if i < len(x) and i < len(y) else (x[i] if i < len(x) else y[i])
            for i in range(max(len(x), len(y)))
        ]

    alpha, beta = [weight], []
    sigma = [weight]
    alphas, betas, sigmas = [], [], []
    for _ in range(steps):
        sigmas.append(sigma)
        alpha = [damp * x for x in sigma]
        raised = [jnp.zeros_like(weight)] + sigma
        beta = add(add(beta, [vertical(x) for x in sigma]), raised)
        sigma = add(alpha, beta)
        alphas.append(alpha)
        betas.append(beta)
    slots = [(s, k) for s in range(1, steps + 1) for k in range(s)]
    place = {key: n for n, key in enumerate(slots)}
    on_disp, on_mom = [], []
    count = 0
    for s, k in slots:
        weights[count] = betas[s - 1][k]
        on_disp.append((count, place[s, k]))
        count += 1
        if k < s - 1:
            weights[count] = alphas[s - 1][k]
            on_mom.append((count, place[s, k]))
            count += 1
    weights[count] = weight
    on_disp.append((count, len(slots)))
    weights[count + 1] = damp * weight
    on_mom.append((count + 1, len(slots) + 1))
    gamma_place = {}
    for j in range(steps):
        for k in range(j + 1):
            n = len(gamma_place)
            gamma_place[j, k] = n
            gammas[pl.ds(n, 1), :] = sigmas[j][k][levels - 1 : levels]

    load_eta.wait()
    load_flow.wait()
    n_acc = len(slots) + 2
    zero_tile = jnp.zeros((SUB, LANES), f32)
    for j in range(blocks):
        for n in range(len(slots) + 1):
            fields[n, j, pl.ds(rows, RING - rows), :] = jnp.zeros((RING - rows, LANES), f32)
    for r in range(rows // SUB):
        tile_rows = pl.ds(r * SUB, SUB)

        def contract(level, acc, tile_rows=tile_rows):
            acc = list(acc)
            d = [disp[level, tile_rows, pl.ds(j * LANES, LANES)] for j in range(blocks)]
            m = [mom[level, tile_rows, pl.ds(j * LANES, LANES)] for j in range(blocks)]
            for source, table in ((d, on_disp), (m, on_mom)):
                for row, target in table:
                    w = jnp.broadcast_to(weights[row, pl.ds(level, 1), :], (SUB, LANES))
                    for j in range(blocks):
                        n = target * blocks + j
                        acc[n] = acc[n] + w * source[j]
            return tuple(acc)

        acc = lax.fori_loop(0, levels, contract, (zero_tile,) * (n_acc * blocks), unroll=2)
        for j in range(blocks):
            shared = acc[(len(slots) + 1) * blocks + j]
            for s, k in slots:
                value = acc[place[s, k] * blocks + j]
                fields[place[s, k], j, tile_rows, :] = value + shared if k == s - 1 else value
            fields[len(slots), j, tile_rows, :] = acc[len(slots) * blocks + j]

    load_cell.wait()
    pick = jnp.where(
        lax.broadcasted_iota(jnp.int32, (SUB, tiles), 1) == own, f32(1.0), f32(0.0)
    ).astype(jnp.bfloat16)
    shift = (blocks * LANES).bit_length() - 1
    columns = lax.broadcasted_iota(jnp.int32, (blocks * LANES, LANES), 0).astype(f32)
    for i in range(half):
        sources = []
        for h in range(2):
            sources.append(cell_buf[:, h * half + i, :])
            if tiles < SLOTS:
                sources.append(jnp.zeros((SLOTS - tiles, tiles), jnp.int32))
        cell = jnp.concatenate(sources, axis=0)
        column = cell & (blocks * LANES - 1)
        digits = [cell >> shift, column >> 7, column & (LANES - 1)]
        digits = jnp.concatenate([x.astype(f32) for x in digits], axis=0).astype(jnp.bfloat16)
        found = lax.dot_general(
            pick, digits, (((1,), (1,)), ((), ())), preferred_element_type=f32
        )
        places[pl.ds(half + i, 1), :] = found[:1, :LANES]
        places[pl.ds(i, 1), :] = found[:1, LANES : 2 * LANES] * LANES + found[:1, 2 * LANES :]

    def expand_columns(i, carry):
        lanes = pl.ds(pl.multiple_of(i * LANES, LANES), LANES)
        match = columns == places[pl.ds(i, 1), :]
        onehot_col[:, lanes] = jnp.where(match, f32(1.0), f32(0.0)).astype(jnp.bfloat16)
        return carry

    lax.fori_loop(0, half, expand_columns, 0, unroll=2)

    @pl.when(jnp.logical_not(hurry))
    def _():
        exchange()

    pl.semaphore_wait(half_in, 1)
    tell(beside_in, before, win)
    tell(beside_in, after, win)
    to_before.wait_recv()
    to_after.wait_recv()
    sub = lax.broadcasted_iota(jnp.int32, (SUB, LANES), 0)
    lane = lax.broadcasted_iota(jnp.int32, (SUB, LANES), 1)
    for j in range(blocks):
        lanes = pl.ds(j * LANES, LANES)
        depth_ring[j, pl.ds(0, rows), :] = depth_own[:, lanes]
        depth_ring[j, pl.ds(rows, SUB), :] = jnp.where(
            sub < reach, depth_low[:, lanes], depth_high[:, lanes]
        )
    for k in range(PHASES):
        ring_row = sub * PHASES + k
        first = jnp.where(own == 0, 0, 1)
        last = jnp.where(own == tiles - 1, 0, 1)
        valid = jnp.where(ring_row < rows, 1, jnp.where(ring_row < rows + reach, last, first))
        for j in range(blocks):
            classes = depth_ring[j, pl.ds(k, SUB, stride=PHASES), :]
            value = jnp.zeros((SUB, LANES), f32)
            for index in range(speed.shape[0]):
                value = jnp.where(classes == index, speed[index], value)
            celerity[j, k] = jnp.where(valid == 1, value, f32(0.0))

    at_left = lane == 0
    at_right = lane == LANES - 1
    scale = f32(1.0 / math.sqrt(levels))

    def laplace(x):
        result = [[None] * PHASES for _ in range(blocks)]
        for k in range(PHASES):
            turned = [pltpu.roll(x[j][k], 1, axis=1) for j in range(blocks)]
            back = [pltpu.roll(x[j][k], LANES - 1, axis=1) for j in range(blocks)]
            for j in range(blocks):
                left = jnp.where(at_left, turned[j - 1] if j > 0 else f32(0.0), turned[j])
                right = jnp.where(
                    at_right, back[j + 1] if j < blocks - 1 else f32(0.0), back[j]
                )
                up = x[j][k - 1] if k > 0 else pltpu.roll(x[j][PHASES - 1], 1, axis=0)
                down = x[j][k + 1] if k < PHASES - 1 else pltpu.roll(x[j][0], SUB - 1, axis=0)
                around = (left + right) + (up + down)
                result[j][k] = celerity[j, k] * (around - 4.0 * x[j][k])
        return result

    def field(n):
        return [
            [fields[n, j, pl.ds(k, SUB, stride=PHASES), :] for k in range(PHASES)]
            for j in range(blocks)
        ]

    def plus(x, y):
        return [[x[j][k] + y[j][k] for k in range(PHASES)] for j in range(blocks)]

    top = laplace(field(len(slots)))
    for s in range(1, steps + 1):
        value = plus(field(place[s, s - 1]), top)
        for power in range(s - 2, -1, -1):
            value = plus(field(place[s, power]), laplace(value))
        for j in range(blocks):
            for k in range(PHASES):
                from_state[s - 1, j, k] = value[j][k]

    pltpu.make_async_copy(
        recv.at[pl.ds(0, tiles - 1)], recv.at[pl.ds(0, tiles - 1)], res_recv
    ).wait()
    values = recv[:, 0, :]
    values = jnp.transpose(
        jnp.concatenate([values, pltpu.roll(values, LANES // 2, axis=1)], axis=0)
    )
    cols[...] = values[: steps * half]
    ring_rows = [(sub * PHASES + k).astype(f32) for k in range(PHASES)]

    def expand(i, carry):
        lanes = pl.ds(pl.multiple_of(i * LANES, LANES), LANES)
        row = places[pl.ds(half + i, 1), :]
        match = [row == ring_rows[k] for k in range(PHASES)]
        high, low = [], []
        for t in range(steps):
            value = cols[pl.ds(t * half + i, 1), :]
            coarse = value.astype(jnp.bfloat16).astype(f32)
            fine = value - coarse
            for k in range(PHASES):
                high.append(jnp.where(match[k], coarse, f32(0.0)))
                low.append(jnp.where(match[k], fine, f32(0.0)))
        onehot_row[:, lanes] = jnp.concatenate(high + low, axis=0).astype(jnp.bfloat16)
        return carry

    lax.fori_loop(0, half, expand, 0, unroll=8)
    product = lax.dot_general(
        onehot_row[...],
        onehot_col[...],
        (((1,), (1,)), ((), ())),
        preferred_element_type=f32,
    )
    inject[...] = product[: steps * RING] + product[steps * RING :]

    def source(s, power):
        value = [[None] * PHASES for _ in range(blocks)]
        for n in range(1, s - power + 1):
            g = gammas[pl.ds(gamma_place[s - n, power], 1), :]
            t = steps - n
            for j in range(blocks):
                for k in range(PHASES):
                    term = g * inject[
                        pl.ds((t * PHASES + k) * SUB, SUB), pl.ds(j * LANES, LANES)
                    ]
                    value[j][k] = term if value[j][k] is None else value[j][k] + term
        return value

    for s in range(1, steps + 1):
        value = source(s, s - 1)
        for power in range(s - 2, -1, -1):
            value = plus(source(s, power), laplace(value))
        t = steps - s
        for j in range(blocks):
            for k in range(PHASES):
                send_rows[pl.ds(k * part + t * blocks + j, SUB, stride=PHASES * part), :] = (
                    value[j][k] + from_state[s - 1, j, k]
                ) * scale

    slot_rows = pl.ds(pl.multiple_of(win * part, part), part)
    edge_copies = []
    for i in range(reach):
        size = part if i < reach // 2 else part // 2
        slot_part = pl.ds(pl.multiple_of(win * part, part), size)
        for ring_row, tile, target in (
            (rows + i, after, i),
            (RING - 1 - i, before, rows - 1 - i),
        ):
            edge_copies.append(
                pltpu.make_async_remote_copy(
                    src_ref=send_rows.at[pl.ds(ring_row * part, size)],
                    dst_ref=edge_in.at[slot_part],
                    send_sem=edge_send.at[len(edge_copies)],
                    recv_sem=edge_recv,
                    device_id={"trench": tile, "tblock": target},
                    device_id_type=MESH,
                )
            )
    def send_row(target):
        pltpu.make_async_remote_copy(
            src_ref=send_rows.at[pl.ds(pl.multiple_of(target * part, part), part)],
            dst_ref=rows_in.at[slot_rows],
            send_sem=row_send,
            recv_sem=row_recv,
            device_id={"trench": own, "tblock": target},
            device_id_type=MESH,
        ).start()

    def send_far(i, carry):
        send_row((1 - my_side) * side + lax.rem(my_place + side // 2 + i, side))
        return carry

    def send_near(i, carry):
        send_row(my_side * side + lax.rem(my_place + i, side))
        return carry

    lax.fori_loop(0, side, send_far, 0)
    pl.semaphore_wait(beside_in, 2)
    for copy in edge_copies:
        copy.start()
    lax.fori_loop(1, side, send_near, 0)
    rows_in[slot_rows, :] = send_rows[slot_rows, :]

    pltpu.make_async_copy(
        rows_in.at[pl.ds(0, (windows - 1) * part)],
        rows_in.at[pl.ds(0, (windows - 1) * part)],
        row_recv,
    ).wait()

    @pl.when((win < reach // 2) | (win >= rows - reach // 2))
    def _():
        pltpu.make_async_copy(edge_in, edge_in, edge_recv).wait()

    @pl.when(
        ((win >= reach // 2) & (win < reach))
        | ((win < rows - reach // 2) & (win >= rows - reach))
    )
    def _():
        whole = edge_in.at[pl.ds(0, windows * part // 2)]
        pltpu.make_async_copy(whole, whole, edge_recv).wait()

    length = windows * part
    total[pl.ds(0, length), :] = rows_in[...] + edge_in[...]
    total[pl.ds(length, TAIL), :] = jnp.zeros((TAIL, LANES), f32)

    to_before.wait_send()
    to_after.wait_send()
    pltpu.make_async_copy(
        msg.at[pl.ds(0, tiles - 1)], msg.at[pl.ds(0, tiles - 1)], res_send
    ).wait()
    pltpu.make_async_copy(
        send_rows.at[pl.ds(0, (windows - 1) * part)],
        send_rows.at[pl.ds(0, (windows - 1) * part)],
        row_send,
    ).wait()
    for copy in edge_copies:
        copy.wait_send()


def prior(blocks, length, total, band, out):
    result = band[0] * total[pl.ds(0, length), :]
    for offset in range(1, band.shape[0]):
        result = result + band[offset] * total[pl.ds(offset * blocks, length), :]
    out[...] = result


def body(
    tiles,
    windows,
    adjoint_eta,
    adjoint_flow,
    residual,
    sensor_cell,
    sensor_count,
    depth_class,
    speed_table,
    damping,
    profile,
    band_weight,
):
    levels, rows, across = adjoint_eta.shape[1:]
    steps, cap = residual.shape[3:]
    blocks = across // LANES
    part = steps * blocks
    length = windows * part
    f32, i32 = jnp.float32, jnp.int32
    padded = (levels // SUB + 1) * SUB
    pairs = steps * (steps + 1) // 2
    by_owner = jnp.transpose(residual[0, 0], (1, 2, 0)).reshape(steps * cap, tiles)
    cells = jnp.transpose(sensor_cell, (0, 2, 1))
    hbm = pl.BlockSpec(memory_space=pltpu.HBM)
    vmem = pl.BlockSpec(memory_space=pltpu.VMEM)
    smem = pl.BlockSpec(memory_space=pltpu.SMEM)
    dma = pltpu.SemaphoreType.DMA
    total = pl.pallas_call(
        functools.partial(kernel, (tiles, windows, levels, rows, blocks, steps, cap)),
        out_shape=jax.ShapeDtypeStruct((length + TAIL, LANES), f32),
        in_specs=[hbm] * 9,
        out_specs=vmem,
        scratch_shapes=[
            pltpu.VMEM(sensor_count.shape, i32),
            pltpu.SMEM(speed_table.shape, f32),
            pltpu.SMEM(damping.shape, f32),
            pltpu.SMEM(profile.shape, f32),
            pltpu.VMEM((levels, rows, across), f32),
            pltpu.VMEM((levels, rows, across), f32),
            pltpu.VMEM((2, padded, LANES), f32),
            pltpu.VMEM((pairs + (steps - 1) * steps // 2 + 2, padded, LANES), f32),
            pltpu.VMEM((2 * SUB, LANES), f32),
            pltpu.VMEM((pairs + 1, blocks, RING, LANES), f32),
            pltpu.VMEM((steps * cap, tiles), f32),
            pltpu.VMEM((tiles, cap, tiles), i32),
            pltpu.VMEM((rows, across), i32),
            pltpu.VMEM((SUB, across), i32),
            pltpu.VMEM((SUB, across), i32),
            pltpu.VMEM((blocks, RING, LANES), i32),
            pltpu.VMEM((blocks, PHASES, SUB, LANES), f32),
            pltpu.VMEM((tiles, 1, LANES), f32),
            pltpu.VMEM((SLOTS, 1, LANES), f32),
            pltpu.VMEM((2 * steps * RING, SLOTS * cap), jnp.bfloat16),
            pltpu.VMEM((across, SLOTS * cap), jnp.bfloat16),
            pltpu.VMEM((cap, LANES), f32),
            pltpu.VMEM((steps * cap // 2, LANES), f32),
            pltpu.VMEM((steps * RING, across), f32),
            pltpu.VMEM((steps, blocks, PHASES, SUB, LANES), f32),
            pltpu.VMEM((RING * part, LANES), f32),
            pltpu.VMEM((length, LANES), f32),
            pltpu.VMEM((length, LANES), f32),
            dma((9,)),
            dma((2,)),
            dma((2,)),
            dma,
            dma,
            dma,
            dma,
            dma((2 * steps,)),
            dma,
            pltpu.SemaphoreType.REGULAR,
            pltpu.SemaphoreType.REGULAR,
        ],
        compiler_params=pltpu.CompilerParams(
            collective_id=0, has_side_effects=True, vmem_limit_bytes=56 << 20
        ),
        name="adjoint",
    )(
        adjoint_eta[0],
        adjoint_flow[0],
        by_owner,
        cells,
        sensor_count,
        depth_class,
        speed_table,
        damping,
        profile,
    )
    result = pl.pallas_call(
        functools.partial(prior, blocks, length),
        out_shape=jax.ShapeDtypeStruct((length, LANES), f32),
        in_specs=[vmem, smem],
        out_specs=vmem,
        name="prior",
    )(total, band_weight)
    return result.reshape(windows * steps, 1, across)


def solution(mesh):
    in_specs = (
        P("tblock", None, "trench", None),
        P("tblock", None, "trench", None),
        P("tblock", "trench", None, None, None),
        P(),
        P(),
        P("trench", None),
        P(),
        P(),
        P(),
        P(),
    )
    out_specs = P(None, ("trench", "tblock"), None)
    sizes = mesh.shape
    return jax.shard_map(
        functools.partial(body, sizes["trench"], sizes["tblock"]),
        mesh=mesh,
        in_specs=in_specs,
        out_specs=out_specs,
        check_vma=False,
    )
```
